256 devices in a mesh: wide: 64 (over y, z, core), narrow: 4 (over x).
Axes of the slice: x: 4, y: 4, z: 8, core: 2. Of those that a mesh axis runs over, the one named last changes fastest.
Arguments:
- patches: bfloat16 [65536, 1280], P('wide', 'narrow'), may hold values from -6 to 6
- norm_gain: float32 [1280], replicated, may hold values from 0.1 to 1.9
- norm_bias: float32 [1280], replicated, may hold values from -3 to 3
- w_in: bfloat16 [1280, 5120], P('wide', 'narrow'), may hold values from -0.15625 to 0.15625
- b_in: float32 [5120], P('narrow'), may hold values from -3 to 3
- w_out: bfloat16 [5120, 1280], P('narrow', 'wide'), may hold values from -0.078125 to 0.078125
- b_out: float32 [1280], P('narrow'), may hold values from -3 to 3
- w_proj: bfloat16 [4, 1280, 1280], P(None, 'narrow', 'wide'), may hold values from -0.078125 to 0.078125
- b_proj: float32 [1280], P('narrow'), may hold values from -3 to 3
- text: bfloat16 [32768, 1280], P('wide', 'narrow'), may hold values from -6 to 6
- place: int32 [16384], replicated, may hold values from -1 to 32767, as said below
Outputs:
- prompt_embeds: bfloat16 [32768, 1280], P('wide', 'narrow')
The draws below stay inside these ranges and needn't reach their ends.
Inputs may be any that keep to these rules, and one draw needn't show every extreme that they name: `place`: of the 256 entries of one wide index (entries i * 256 to (i + 1) * 256 - 1), the valid ones (>= 0) come first and -1 fills the rest; three quarters or more are valid, and all are valid for some wide index. Valid values are distinct. For one wide index, at most 8 valid entries v have the same v // 512, and every wide index reaches 8 for some value.
All inputs are finite; a program needn't handle non-finite values.
Results may differ from the reference program's by a relative error of at most 0.012.
Values may be sent and summed in bfloat16 or wider, within the bound.
A program may use at most 64 MiB of HBM per device.

```python
import jax
import jax.numpy as jnp
from jax import lax

D = 1280
FF = 5120
DL = 1280
TOK_GROUP = 1024
MERGE_ROWS = 256
SEQ_GROUP = 512
BUCKET = 8
TOKENS = 65536
MERGED = 16384
SEQ_LEN = 32768
N_WIDE = 64
N_NARROW = 4


def draw_place(key, part):
    groups = MERGED // MERGE_ROWS
    slot_count = BUCKET * groups
    key_pad, key_full, key_slot, key_row, key_pos = jax.random.split(key, 5)
    padding = jax.random.randint(key_pad, (groups,), 0, MERGE_ROWS // 4 + 1)
    fullest = jax.random.randint(key_full, (), 0, groups)
    padding = jnp.where(jnp.arange(groups) == fullest, 0, padding)
    counts = MERGE_ROWS - padding

    def slot_order(subkey):
        shuffled = jax.random.permutation(subkey, slot_count)
        hottest = shuffled[0] // BUCKET
        order_rank = jnp.argsort(shuffled)
        scores = jnp.where(jnp.arange(slot_count) // BUCKET == hottest, 0, slot_count) + order_rank
        return jnp.argsort(scores)[:MERGE_ROWS]

    def row_order(subkey, row_count):
        order_rank = jnp.argsort(jax.random.permutation(subkey, MERGE_ROWS))
        positions = jnp.arange(MERGE_ROWS)
        return jnp.argsort(jnp.where(positions < row_count, order_rank, MERGE_ROWS + positions))

    def layout_order(subkey):
        return jax.random.permutation(subkey, SEQ_GROUP)
    chosen = jax.vmap(slot_order)(jax.random.split(key_slot, groups))
    row_perm = jax.vmap(row_order)(jax.random.split(key_row, groups), counts)
    slot_of_row = jnp.take_along_axis(chosen, row_perm, axis=1)
    target = slot_of_row // BUCKET
    within = slot_of_row % BUCKET
    layouts = jax.vmap(layout_order)(jax.random.split(key_pos, groups))
    source = jnp.arange(groups)[:, None]
    local_row = layouts[target, source * BUCKET + within]
    placed = target * SEQ_GROUP + local_row
    is_valid = jnp.arange(MERGE_ROWS)[None, :] < counts[:, None]
    return jnp.where(is_valid, placed, -1).reshape(-1).astype(jnp.int32)


def block_scale(key, extent, cuts, smallest, high):
    gain = 1.0
    for axis_at, shards_of in cuts:
        steps = jax.random.uniform(jax.random.fold_in(jax.random.fold_in(key, 6), axis_at), (shards_of,), jnp.float32, smallest / len(cuts), high / len(cuts))
        gain = gain * jnp.repeat(jnp.exp(steps), extent[axis_at] // shards_of).reshape((-1,) + (1,) * (len(extent) - 1 - axis_at))
    return gain


def scatter_about(rng, extent, scale, limit, cuts=(), kind=jnp.bfloat16):
    entries = jax.random.normal(rng, extent, jnp.float32) * scale
    if len(cuts) > 0:
        entries = block_scale(rng, extent, cuts, -0.22, 0.18) * entries
    return jnp.clip(entries, min=-limit, max=limit).astype(kind)


def setup_inputs(seed: int = 0) -> dict:
    seeds = jax.random.split(jax.random.key(seed), 12)
    return {
        "patches": scatter_about(seeds[0], (TOKENS, D), 1.0, 6.0, ((0, 64), (1, 4))),
        "norm_gain": jnp.clip(1.0 + 0.18 * jax.random.normal(seeds[1], (D,), jnp.float32), 0.1, 1.9),
        "norm_bias": scatter_about(seeds[2], (D,), 0.5, 3.0, (), jnp.float32),
        "w_in": scatter_about(seeds[3], (D, FF), D ** -0.5, 0.15625, ((0, 64), (1, 4))),
        "b_in": scatter_about(seeds[4], (FF,), 0.5, 3.0, ((0, 4),), jnp.float32),
        "w_out": scatter_about(seeds[5], (FF, D), FF ** -0.5, 0.078125, ((0, 4), (1, 64))),
        "b_out": scatter_about(seeds[6], (D,), 0.5, 3.0, ((0, 4),), jnp.float32),
        "w_proj": scatter_about(seeds[7], (4, D, DL), (4 * D) ** -0.5, 0.078125, ((1, 4), (2, 64))),
        "b_proj": scatter_about(seeds[8], (DL,), 0.5, 3.0, ((0, 4),), jnp.float32),
        "text": scatter_about(seeds[9], (SEQ_LEN, DL), 1.0, 6.0, ((0, 64), (1, 4))),
        "place": draw_place(jax.random.fold_in(seeds[11], 71), 0),
    }


def block_sums(left, right):
    width = left.shape[1] // N_NARROW
    total = jnp.zeros((left.shape[0], right.shape[1]), jnp.float32)
    for block in range(N_NARROW):
        term = jnp.dot(left[:, block * width:(block + 1) * width], right[block * width:(block + 1) * width], preferred_element_type=jnp.float32).astype(jnp.bfloat16)
        term = lax.optimization_barrier(term)
        total = total + term.astype(jnp.float32)
    return total

def encode_group(group_rows, norm_gain, norm_bias, w_in, b_in, w_out, b_out, w_proj, b_proj):
    values = group_rows.astype(jnp.float32)
    center = lax.optimization_barrier(jnp.mean(values, axis=-1, keepdims=True))
    spread = lax.optimization_barrier(jnp.mean(jnp.square(values - center), axis=-1, keepdims=True))
    normed = ((values - center) * lax.rsqrt(spread + 1e-06) * norm_gain + norm_bias).astype(jnp.bfloat16)
    product = jnp.dot(normed, w_in, preferred_element_type=jnp.float32) + b_in
    hidden = jax.nn.gelu(product, approximate=False).astype(jnp.bfloat16)
    mlp_out = block_sums(hidden, w_out) + b_out
    stream = (values + mlp_out).astype(jnp.bfloat16)
    window_rows = stream.shape[0] // 4
    width = D // N_NARROW
    windows = stream.reshape(window_rows, 4, N_NARROW, width).transpose(0, 2, 1, 3).reshape(window_rows, N_NARROW * 4 * width)
    proj_rows = w_proj.reshape(4, N_NARROW, width, DL).transpose(1, 0, 2, 3).reshape(N_NARROW * 4 * width, DL)
    vision = block_sums(windows, proj_rows) + b_proj
    return vision.astype(jnp.bfloat16)

def reference(patches, norm_gain, norm_bias, w_in, b_in, w_out, b_out, w_proj, b_proj, text, place):
    grouped = patches.reshape(N_WIDE, TOK_GROUP, D)

    def one_group(group_rows):
        return encode_group(group_rows, norm_gain, norm_bias, w_in, b_in, w_out, b_out, w_proj, b_proj)
    vision = lax.map(one_group, grouped).reshape(MERGED, DL)
    target = jnp.where(place >= 0, place, SEQ_LEN).astype(jnp.int32)
    return text.at[target].set(vision, mode='drop')
```

```python
import jax
import jax.numpy as jnp
from jax import lax
from jax.sharding import PartitionSpec as P


def select_rows(index, rows, count):
    pick = (jnp.arange(count, dtype=jnp.int32)[:, None] == index[None, :]).astype(rows.dtype)
    return jnp.dot(pick, rows, preferred_element_type=jnp.float32).astype(rows.dtype)


def per_device(
    patches, norm_gain, norm_bias, w_in, b_in, w_out, b_out, w_proj, b_proj, text, place
):
    groups = lax.axis_size("wide")
    width = w_in.shape[0]
    local = jnp.concatenate(
        [w_in, w_out.T, w_proj.transpose(2, 0, 1).reshape(width, -1)], axis=0
    )
    gathered = lax.all_gather(local, "wide", axis=0, tiled=False)
    rows_in = gathered[:, :width].reshape(groups * width, -1)
    cols_out = gathered[:, width : 2 * width].reshape(groups * width, -1)
    proj_cols = gathered[:, 2 * width :].reshape(groups * width, -1)

    whole = lax.all_gather(patches, "narrow", axis=1, tiled=True)
    values = whole.astype(jnp.float32)
    center = jnp.mean(values, axis=-1, keepdims=True)
    spread = jnp.mean(jnp.square(values - center), axis=-1, keepdims=True)
    normed = ((values - center) * lax.rsqrt(spread + 1e-06) * norm_gain + norm_bias).astype(
        jnp.bfloat16
    )
    product = jnp.dot(normed, rows_in, preferred_element_type=jnp.float32)
    hidden = jax.nn.gelu(product + b_in, approximate=False).astype(jnp.bfloat16)
    partial_out = lax.dot_general(
        hidden, cols_out, (((1,), (1,)), ((), ())), preferred_element_type=jnp.float32
    )
    mlp_out = lax.psum_scatter(
        partial_out.astype(jnp.bfloat16), "narrow", scatter_dimension=1, tiled=True
    ).astype(jnp.float32)
    stream = (patches.astype(jnp.float32) + (mlp_out + b_out)).astype(jnp.bfloat16)
    merge_count = stream.shape[0] // 4
    merged = stream.reshape(merge_count, 4 * stream.shape[1])
    own_index = lax.axis_index("wide")
    seq_rows = text.shape[0]
    bucket = seq_rows // groups
    place_table = place.reshape(groups, merge_count)
    owners = jnp.where(place_table >= 0, place_table // seq_rows, groups)
    own_owners = lax.dynamic_index_in_dim(owners, own_index, 0, keepdims=False)
    owner_hits = (own_owners[:, None] == jnp.arange(groups, dtype=jnp.int32)[None, :]).astype(
        jnp.int32
    )
    slot_out = jnp.sum(jnp.cumsum(owner_hits, axis=0) * owner_hits, axis=1) - 1
    send_row = jnp.where(
        (own_owners < groups) & (slot_out < bucket), own_owners * bucket + slot_out, -1
    )
    arriving = owners == own_index
    slot_in = jnp.cumsum(arriving.astype(jnp.int32), axis=1) - 1
    slot_in = jnp.where(arriving, slot_in, bucket)
    local_row = place_table % seq_rows
    slot_hits = slot_in[:, :, None] == jnp.arange(bucket, dtype=jnp.int32)[None, None, :]
    targets = jnp.sum(jnp.where(slot_hits, local_row[:, :, None] + 1, 0), axis=1) - 1
    partial_proj = lax.dot_general(
        merged, proj_cols, (((1,), (1,)), ((), ())), preferred_element_type=jnp.float32
    )
    vision = (
        lax.psum_scatter(
            partial_proj.astype(jnp.bfloat16), "narrow", scatter_dimension=1, tiled=True
        ).astype(jnp.float32)
        + b_proj
    ).astype(jnp.bfloat16)
    outgoing = select_rows(send_row, vision, groups * bucket).reshape(groups, bucket, -1)
    received = lax.all_to_all(outgoing, "wide", split_axis=0, concat_axis=0, tiled=True)
    flat_targets = targets.reshape(-1)
    placed = select_rows(flat_targets, received.reshape(-1, received.shape[2]), seq_rows)
    hit = jnp.any(
        jnp.arange(seq_rows, dtype=jnp.int32)[:, None] == flat_targets[None, :], axis=1
    )
    return jnp.where(hit[:, None], placed, text)


def solution(mesh):
    placed = (
        P("wide", "narrow"),
        P(),
        P(),
        P("wide", "narrow"),
        P("narrow"),
        P("narrow", "wide"),
        P("narrow"),
        P(None, "narrow", "wide"),
        P("narrow"),
        P("wide", "narrow"),
        P(),
    )
    return jax.shard_map(
        per_device, mesh=mesh, in_specs=placed, out_specs=P("wide", "narrow"), check_vma=False
    )
```
